512 devices in a mesh: dp: 16 (over z, core), cls: 32 (over x, y).
Axes of the slice: x: 4, y: 8, z: 8, core: 2. Of those that a mesh axis runs over, the one named last changes fastest.
Arguments:
- embeddings: bfloat16 [131072, 768], P(('dp', 'cls'))
- class_rows: bfloat16 [128, 256, 768], P('cls')
- cand_blocks: int32 [1024, 8], P(('dp', 'cls')), may hold values from 0 to 127, all different within a row; in each aligned block of 64 rows (0 to 63, 64 to 127, ...) at most 8 rows name the same one
- label_pos: int32 [131072], P(('dp', 'cls')), may hold values from 0 to 2047
Outputs:
- image_loss: float32 [131072], P('dp')
- class_grad: float32 [256, 128, 768], P('dp', 'cls')
The draws below stay inside these ranges and needn't reach their ends.
Inputs may be any that keep to these rules, and one draw needn't show every extreme that they name: `cand_blocks`: the 8 blocks of one list differ; block n lives on index n // 4 of cls. Among the 64 lists of one index of dp no block is named by more than 8 lists, and in some index of dp one block is named by exactly 8.
All inputs are finite; a program needn't handle non-finite values.
Results may differ from the reference program's by a relative error of at most 0.00099.
Values may be sent and summed in bfloat16 or wider, within the bound.
A program may use at most 64 MiB of HBM per device.

```python
import math
import jax
import jax.numpy as jnp
import numpy as np
from jax import lax

D = 768
TB = 256
IMG_BLK = 128
K = 8
BLK_DEV = 4
IMG_DEV = 256
NBLK = 128
IMGS = 131072
NIB = 1024
MOST = 8
N_CLS = 32


def draw_class_rows(key, part):
    spread = 3.0 / math.sqrt(D)
    base_rows = jnp.clip(jax.random.normal(jax.random.fold_in(key, 12), (NBLK, TB, D), jnp.float32), -6.0, 6.0) * spread
    return base_rows.astype(jnp.bfloat16)


def draw_embeddings(key, part):
    values = jnp.clip(jax.random.normal(jax.random.fold_in(key, 21), (IMGS, D), jnp.float32), -6.0, 6.0)
    return values.astype(jnp.bfloat16)


def with_ends(drawn, stream_key, low, largest):
    dims = drawn.shape
    spot = [jax.random.randint(jax.random.fold_in(stream_key, axis), (), 0, dims[axis]) for axis in range(len(dims))]
    drawn = drawn.at[tuple(spot)].set(low)
    longest = dims.index(max(dims))
    spot[longest] = (spot[longest] + 1) % dims[longest]
    return drawn.at[tuple(spot)].set(largest)


def shared_out(key, own, number, rows, count, top, bound, slope):
    ranking = jax.random.permutation(key, count)
    packed, common = portions_of(count, rows * top, bound, slope, True), portions_of(count, rows * top, bound, slope, False)
    places = jnp.arange(count)

    def named(lengths, turn):
        used = int((lengths > 0).sum())
        fixed = max(1, used // 4)
        moved = fixed + (places - fixed + turn * (used - fixed)) % max(1, count - fixed)
        return jnp.zeros((count,), jnp.int32).at[ranking[jnp.where(places < fixed, places, moved)]].set(jnp.asarray(lengths, jnp.int32))

    lengths = jnp.where(number % 4 == 0, named(packed, number // 4), named(common, number - number // 4 - 1))
    mixed = jax.random.permutation(jax.random.fold_in(own, 3), count)
    source_of, taker = mixed[0:count // 2 * 2:2], mixed[1:count // 2 * 2:2]
    room = jnp.minimum(lengths[source_of] - 1, bound - lengths[taker]) // 2
    room = jnp.where((source_of == ranking[0]) | (taker == ranking[0]) | (lengths[taker] == 0), 0, jnp.maximum(room, 0))
    moved = jax.random.randint(jax.random.fold_in(own, 4), (count // 2,), 0, 1 << 20) % (room + 1)
    lengths = lengths.at[source_of].add(-moved).at[taker].add(moved)
    items = jnp.searchsorted(jnp.cumsum(lengths), jnp.arange(rows * top), side="right").astype(jnp.int32)
    table = items.reshape(top, rows).T
    table = table[jax.random.permutation(jax.random.fold_in(own, 1), rows)]
    turn = jax.random.randint(jax.random.fold_in(own, 2), (rows, 1), 0, top)
    return jnp.take_along_axis(table, (jnp.arange(top)[None, :] + turn) % top, axis=1)


def portions_of(number_of, total, limit, skew, full):
    portions = [(1 << 20) // math.isqrt(grade ** skew) + 1 for grade in range(1, number_of + 1)]
    largest = limit if full else min(limit, max(-(-total // number_of), total * portions[0] // sum(portions)))
    least = 1 if total - largest >= number_of - 1 else 0
    counts, surplus = [largest] + [least] * (number_of - 1), total - largest - least * (number_of - 1)
    while surplus > 0:
        movable = [i for i in range(1, number_of) if counts[i] < largest] or [i for i in range(1, number_of) if counts[i] < limit]
        whole, left = sum([portions[i] for i in movable]), surplus
        for i in movable:
            addition = min(limit - counts[i], max(1, left * portions[i] // whole), surplus)
            counts[i] = counts[i] + addition
            surplus = surplus - addition
    return np.array(counts)


def setup_inputs(seed: int = 0) -> dict:
    splits = jax.random.split(jax.random.key(seed), 5)
    embeddings = draw_embeddings(jax.random.fold_in(splits[4], 71), 0)
    class_rows = draw_class_rows(jax.random.fold_in(splits[4], 71), 0)
    cand_blocks_keys = jax.random.split(jax.random.fold_in(splits[2], 1), NIB // (IMG_DEV * N_CLS // IMG_BLK))
    cand_blocks_turns = jax.random.permutation(jax.random.fold_in(splits[2], 3), NIB // (IMG_DEV * N_CLS // IMG_BLK))
    cand_blocks = jax.vmap(lambda own, number: shared_out(jax.random.fold_in(splits[2], 2), own, number, IMG_DEV * N_CLS // IMG_BLK, BLK_DEV * N_CLS, K, MOST, 2))(cand_blocks_keys, cand_blocks_turns).reshape((NIB, K))
    label_pos = with_ends(jax.random.randint(splits[3], (IMGS,), 0, K * TB), jax.random.fold_in(splits[3], 1), 0, (K * TB) - 1).astype(jnp.int32)
    return dict(embeddings=embeddings, class_rows=class_rows, cand_blocks=cand_blocks, label_pos=label_pos)


def reference(embeddings, class_rows, cand_blocks, label_pos):
    lists = cand_blocks.shape[0]
    image_groups = embeddings.reshape(lists, IMG_BLK, D)
    label_groups = label_pos.reshape(lists, IMG_BLK)
    positions = jnp.arange(K * TB, dtype=jnp.int32)

    def one_list(grad_total, inputs_now):
        image_rows, cand_row, label_row = inputs_now
        weight_rows = class_rows[cand_row].reshape(K * TB, D)
        score = jnp.dot(image_rows, weight_rows.T, preferred_element_type=jnp.float32)
        score_max = jnp.max(score, axis=1)
        exp_total = jnp.sum(jnp.exp(score - score_max[:, None]), axis=1)
        log_norm = score_max + jnp.log(exp_total)
        is_true = positions[None, :] == label_row[:, None]
        true_score = jnp.sum(jnp.where(is_true, score, jnp.float32(0.0)), axis=1)
        image_loss = log_norm - true_score
        logit_grad = (jnp.exp(score - log_norm[:, None]) - is_true.astype(jnp.float32)).astype(jnp.bfloat16)
        contrib = jnp.dot(logit_grad.T, image_rows, preferred_element_type=jnp.float32).reshape(K, TB, D)
        grad_total = grad_total.at[cand_row].add(contrib)
        return grad_total, image_loss

    start_grad = jnp.zeros((NBLK, TB, D), jnp.float32)
    grad_total, losses = lax.scan(one_list, start_grad, (image_groups, cand_blocks, label_groups))
    return losses.reshape(IMGS), jnp.transpose(grad_total, (1, 0, 2))
```

```python
import jax
import jax.numpy as jnp
from jax import lax
from jax.experimental import pallas as pl
from jax.experimental.pallas import tpu as pltpu
from jax.sharding import PartitionSpec as P

MOST = 8
NEG = -3.0e38
N_CLS = 32


def stats_kernel(stats_ref, out_ref, recv, mine, send_a, recv_a, send_b, recv_b):
    me = lax.axis_index("cls")
    barrier = pltpu.get_barrier_semaphore()

    def greet(step, carry):
        pl.semaphore_signal(barrier, inc=1, device_id={"cls": (me + step) % N_CLS})
        return carry

    lax.fori_loop(1, N_CLS, greet, 0)
    pl.semaphore_wait(barrier, N_CLS - 1)

    def part_copy(step):
        target = (me + step) % N_CLS
        return pltpu.make_async_remote_copy(
            src_ref=stats_ref.at[target],
            dst_ref=recv.at[step],
            send_sem=send_a.at[step],
            recv_sem=recv_a.at[step],
            device_id={"cls": target},
        )

    def start_part(step, carry):
        part_copy(step).start()
        return carry

    def wait_part(step, carry):
        part_copy(step).wait()
        return carry

    lax.fori_loop(1, N_CLS, start_part, 0)
    recv[0] = stats_ref[me]
    lax.fori_loop(1, N_CLS, wait_part, 0)

    parts = recv[...]
    tops = parts[:, 0:2, :]
    top = jnp.max(tops, axis=0)
    total = jnp.sum(jnp.exp(tops - top[None]) * parts[:, 2:4, :], axis=0)
    true_score = jnp.sum(parts[:, 4:6, :], axis=0)
    log_norm = top + jnp.log(total)
    mine[0:2, :] = log_norm
    mine[2:4, :] = log_norm - true_score
    mine[4:8, :] = jnp.zeros((4, 128), jnp.float32)
    out_ref[me] = mine[...]

    def whole_copy(step):
        return pltpu.make_async_remote_copy(
            src_ref=mine,
            dst_ref=out_ref.at[me],
            send_sem=send_b.at[step],
            recv_sem=recv_b.at[step],
            device_id={"cls": (me + step) % N_CLS},
        )

    def start_whole(step, carry):
        whole_copy(step).start()
        return carry

    def wait_whole(step, carry):
        whole_copy(step).wait()
        return carry

    lax.fori_loop(1, N_CLS, start_whole, 0)
    lax.fori_loop(1, N_CLS, wait_whole, 0)


def combine_stats(stats):
    return pl.pallas_call(
        stats_kernel,
        out_shape=jax.ShapeDtypeStruct((N_CLS, 8, 128), jnp.float32),
        in_specs=[pl.BlockSpec(memory_space=pltpu.VMEM)],
        out_specs=pl.BlockSpec(memory_space=pltpu.VMEM),
        scratch_shapes=[
            pltpu.VMEM((N_CLS, 8, 128), jnp.float32),
            pltpu.VMEM((8, 128), jnp.float32),
            pltpu.SemaphoreType.DMA((N_CLS,)),
            pltpu.SemaphoreType.DMA((N_CLS,)),
            pltpu.SemaphoreType.DMA((N_CLS,)),
            pltpu.SemaphoreType.DMA((N_CLS,)),
        ],
        compiler_params=pltpu.CompilerParams(collective_id=0, has_side_effects=True),
        name="stats_combine",
    )(stats)


def body(embeddings, class_rows, cand_blocks, label_pos):
    gathered, cand_all, labels_all = (
        lax.all_gather(embeddings, "cls", axis=0, tiled=True),
        lax.all_gather(cand_blocks, "cls", axis=0, tiled=True),
        lax.all_gather(label_pos, "cls", axis=0, tiled=True),
    )
    local_blocks, block_taxa, feature_width = class_rows.shape
    group_lists = cand_all.shape[0]
    dp_images = gathered.shape[0]
    group_rows = dp_images // group_lists
    my_shard = lax.axis_index("cls")
    owned_ids = my_shard * local_blocks + jnp.arange(local_blocks, dtype=jnp.int32)
    matches = (cand_all[:, :, None] == owned_ids[None, None, :]).astype(jnp.int32)
    hit_count = jnp.sum(matches, axis=1)
    slot_of = jnp.sum(
        matches * jnp.arange(cand_all.shape[1], dtype=jnp.int32)[None, :, None], axis=1
    )
    hit_rank = jnp.cumsum(hit_count, axis=0) - 1
    slot_ids = jnp.arange(MOST, dtype=jnp.int32)
    picked = (
        (hit_count[:, :, None] > 0) & (hit_rank[:, :, None] == slot_ids[None, None, :])
    ).astype(jnp.int32)
    block_index = jnp.arange(group_lists, dtype=jnp.int32)[:, None, None]
    src_block = jnp.sum(picked * block_index, axis=0)
    valid_slot = jnp.sum(picked, axis=0)
    src_slot = jnp.sum(picked * slot_of[:, :, None], axis=0)
    image_tiles = gathered.reshape(group_lists, group_rows, feature_width)[src_block]
    label_tiles = labels_all.reshape(group_lists, group_rows)[src_block]
    scores = jnp.einsum(
        "jsid,jtd->jsit", image_tiles, class_rows, preferred_element_type=jnp.float32
    )
    live_slot = (valid_slot > 0)[:, :, None, None]
    target_pos = (
        src_slot[:, :, None, None] * block_taxa
        + jnp.arange(block_taxa, dtype=jnp.int32)[None, None, None, :]
    )
    is_true = (label_tiles[:, :, :, None] == target_pos) & live_slot
    slot_true = jnp.sum(jnp.where(is_true, scores, 0.0), axis=3)
    slot_max = jnp.max(scores, axis=3)
    slot_sum = jnp.sum(jnp.exp(scores - slot_max[..., None]), axis=3)
    owner_map = picked.reshape(group_lists, local_blocks * MOST)
    owner_float = owner_map.astype(jnp.float32)
    flat_max = slot_max.reshape(local_blocks * MOST, group_rows)
    local_max = jnp.max(jnp.where(owner_map[:, :, None] > 0, flat_max[None, :, :], NEG), axis=1)
    base = local_max[src_block.reshape(-1)]
    scaled = jnp.where(
        valid_slot.reshape(-1, 1) > 0,
        jnp.exp(flat_max - base) * slot_sum.reshape(-1, group_rows),
        0.0,
    )
    sums = jnp.einsum(
        "bq,qi->bi",
        owner_float,
        jnp.concatenate([scaled, slot_true.reshape(-1, group_rows)], axis=1),
        precision=lax.Precision.HIGHEST,
    )
    local_sum, local_true = sums[:, :group_rows], sums[:, group_rows:]
    per = group_lists // N_CLS
    parts = [a.reshape(N_CLS, per, group_rows) for a in (local_max, local_sum, local_true)]
    parts.append(jnp.zeros((N_CLS, 8 - 3 * per, group_rows), jnp.float32))
    combined = combine_stats(jnp.concatenate(parts, axis=1))
    log_norm = combined[:, 0:per].reshape(group_lists, group_rows)
    image_loss = combined[:, per : 2 * per].reshape(dp_images)
    softmax_prob = jnp.exp(scores - log_norm[src_block][:, :, :, None])
    logit_grad = jnp.where(live_slot, softmax_prob - is_true.astype(jnp.float32), 0.0).astype(
        jnp.bfloat16
    )
    class_grad = lax.psum_scatter(
        jnp.einsum("jsit,jsid->tjd", logit_grad, image_tiles, preferred_element_type=jnp.float32),
        "dp",
        scatter_dimension=0,
        tiled=True,
    )
    return (image_loss, class_grad)


def solution(mesh):
    in_specs = (
        P(("dp", "cls"), None),
        P("cls", None, None),
        P(("dp", "cls"), None),
        P(("dp", "cls")),
    )
    out_specs = (P("dp"), P("dp", "cls", None))
    return jax.shard_map(body, mesh=mesh, in_specs=in_specs, out_specs=out_specs, check_vma=False)
```

```python
import jax
import jax.numpy as jnp
from jax import lax
from jax.experimental import pallas as pl
from jax.experimental.pallas import tpu as pltpu
from jax.sharding import PartitionSpec as P

MOST = 8
NEG = -3.0e38
N_CLS = 32


def stats_kernel(stats_ref, out_ref, recv, mine, send_a, recv_a, send_b, recv_b):
    me = lax.axis_index("cls")
    barrier = pltpu.get_barrier_semaphore()

    def greet(step, carry):
        pl.semaphore_signal(barrier, inc=1, device_id={"cls": (me + step) % N_CLS})
        return carry

    lax.fori_loop(1, N_CLS, greet, 0)
    pl.semaphore_wait(barrier, N_CLS - 1)

    def part_copy(step):
        target = (me + step) % N_CLS
        return pltpu.make_async_remote_copy(
            src_ref=stats_ref.at[target],
            dst_ref=recv.at[step],
            send_sem=send_a.at[step],
            recv_sem=recv_a.at[step],
            device_id={"cls": target},
        )

    def start_part(step, carry):
        part_copy(step).start()
        return carry

    def wait_part(step, carry):
        part_copy(step).wait()
        return carry

    lax.fori_loop(1, N_CLS, start_part, 0)
    recv[0] = stats_ref[me]
    lax.fori_loop(1, N_CLS, wait_part, 0)

    parts = recv[...]
    tops = parts[:, 0:2, :]
    top = jnp.max(tops, axis=0)
    total = jnp.sum(jnp.exp(tops - top[None]) * parts[:, 2:4, :], axis=0)
    true_score = jnp.sum(parts[:, 4:6, :], axis=0)
    log_norm = top + jnp.log(total)
    mine[0:2, :] = log_norm
    mine[2:4, :] = log_norm - true_score
    mine[4:8, :] = jnp.zeros((4, 128), jnp.float32)
    out_ref[me] = mine[...]

    def whole_copy(step):
        return pltpu.make_async_remote_copy(
            src_ref=mine,
            dst_ref=out_ref.at[me],
            send_sem=send_b.at[step],
            recv_sem=recv_b.at[step],
            device_id={"cls": (me + step) % N_CLS},
        )

    def start_whole(step, carry):
        whole_copy(step).start()
        return carry

    def wait_whole(step, carry):
        whole_copy(step).wait()
        return carry

    lax.fori_loop(1, N_CLS, start_whole, 0)
    lax.fori_loop(1, N_CLS, wait_whole, 0)


def combine_stats(stats):
    return pl.pallas_call(
        stats_kernel,
        out_shape=jax.ShapeDtypeStruct((N_CLS, 8, 128), jnp.float32),
        in_specs=[pl.BlockSpec(memory_space=pltpu.VMEM)],
        out_specs=pl.BlockSpec(memory_space=pltpu.VMEM),
        scratch_shapes=[
            pltpu.VMEM((N_CLS, 8, 128), jnp.float32),
            pltpu.VMEM((8, 128), jnp.float32),
            pltpu.SemaphoreType.DMA((N_CLS,)),
            pltpu.SemaphoreType.DMA((N_CLS,)),
            pltpu.SemaphoreType.DMA((N_CLS,)),
            pltpu.SemaphoreType.DMA((N_CLS,)),
        ],
        compiler_params=pltpu.CompilerParams(collective_id=0, has_side_effects=True),
        name="stats_combine",
    )(stats)


NX, NY, NZ = 4, 8, 8
A_ROWS = 96


def relay_order(rows):
    rate = 46.0
    rate = rate * 1000.0 / 1536.0
    hop = 1.7
    a_rows, b_rows = A_ROWS, rows - A_ROWS
    free = {"x+": 0.0, "x-": 0.0, "y+": 0.0, "y-": 0.0}
    queue, serial, order = [], 0, []

    def span(kind, u, v):
        size, start = (a_rows, 0) if kind == "A" else (b_rows, a_rows)
        first, second = (u, v) if kind == "A" else (v, u)
        far1, far2 = (NX // 2, NY // 2) if kind == "A" else (NY // 2, NX // 2)
        if abs(first) == far1:
            return (start, size // 2) if first < 0 else (start + size // 2, size // 2)
        if abs(second) == far2:
            return (start, size // 2) if second < 0 else (start + size // 2, size // 2)
        return start, size

    def sends(kind, u, v, came):
        result = []
        first_axis = "x" if kind == "A" else "y"
        for axis in ("x", "y"):
            pos, far = (u, NX // 2) if axis == "x" else (v, NY // 2)
            if axis == first_axis and came is not None and came[0] != first_axis:
                continue
            for sign in ("+", "-"):
                if came is not None and came[0] == axis and came[1] != sign:
                    continue
                new = pos - 1 if sign == "+" else pos + 1
                if abs(new) > far:
                    continue
                if axis != first_axis and abs(new) == far:
                    first, far1 = (u, NX // 2) if kind == "A" else (v, NY // 2)
                    if abs(first) == far1 and (first < 0) != (new < 0):
                        continue
                result.append((axis + sign, (new, v) if axis == "x" else (u, new)))
        result.sort(key=lambda item: item[0][0] != first_axis)
        return result

    def launch(now, kind, u, v, came):
        nonlocal serial
        out = []
        for direction, (nu, nv) in sends(kind, u, v, came):
            start, size = span(kind, nu, nv)
            free[direction] = max(free[direction], now) + size / rate
            queue.append((free[direction] + hop, serial, kind, nu, nv, direction))
            serial += 1
            out.append((direction, nu, nv, start, size))
        return out

    first = [("A", launch(0.0, "A", 0, 0, None)), ("B", launch(0.0, "B", 0, 0, None))]
    while queue:
        queue.sort()
        now, _, kind, u, v, direction = queue.pop(0)
        start, size = span(kind, u, v)
        order.append((kind, u, v, start, size, launch(now, kind, u, v, direction)))
    return first, order


def gather_kernel(own_ref, small_ref, out_ref, small_out, send, recv, local, small_send, small_recv):
    me = lax.axis_index("cls")
    x, y = me // NY, me % NY
    barrier = pltpu.get_barrier_semaphore()

    def greet(step, carry):
        pl.semaphore_signal(barrier, inc=1, device_id={"cls": (me + step) % N_CLS})
        return carry

    lax.fori_loop(1, N_CLS, greet, 0)
    pl.semaphore_wait(barrier, N_CLS - 1)

    rows = own_ref.shape[0]
    first, order = relay_order(rows)
    near = {
        "x+": ((x + 1) % NX) * NY + y,
        "x-": ((x + NX - 1) % NX) * NY + y,
        "y+": x * NY + (y + 1) % NY,
        "y-": x * NY + (y + NY - 1) % NY,
    }
    number = {(kind, u, v): i for i, (kind, u, v, _, _, _) in enumerate(order)}
    sent = []

    def slot_of(u, v):
        return ((x + u + NX) % NX) * NY + (y + v + NY) % NY

    def begin(kind, u, v, outs):
        slot = slot_of(u, v)
        for direction, nu, nv, start, size in outs:
            index = number[(kind, nu, nv)]
            source = own_ref if (u, v) == (0, 0) else out_ref.at[slot]
            copy = pltpu.make_async_remote_copy(
                src_ref=source.at[pl.ds(start, size)],
                dst_ref=out_ref.at[slot, pl.ds(start, size)],
                send_sem=send.at[index],
                recv_sem=recv.at[index],
                device_id={"cls": near[direction]},
            )
            copy.start()
            sent.append(copy)

    def small_copy(step):
        return pltpu.make_async_remote_copy(
            src_ref=small_ref,
            dst_ref=small_out.at[me],
            send_sem=small_send.at[step],
            recv_sem=small_recv.at[step],
            device_id={"cls": (me + step) % N_CLS},
        )

    def start_small(step, carry):
        small_copy(step).start()
        return carry

    def wait_small(step, carry):
        small_copy(step).wait()
        return carry

    for kind, outs in first:
        begin(kind, 0, 0, outs)
    lax.fori_loop(1, N_CLS, start_small, 0)
    own = pltpu.make_async_copy(own_ref, out_ref.at[me], local.at[0])
    own.start()
    small_own = pltpu.make_async_copy(small_ref, small_out.at[me], local.at[1])
    small_own.start()
    for index, (kind, u, v, start, size, outs) in enumerate(order):
        pltpu.make_async_remote_copy(
            src_ref=own_ref.at[pl.ds(start, size)],
            dst_ref=out_ref.at[slot_of(u, v), pl.ds(start, size)],
            send_sem=send.at[index],
            recv_sem=recv.at[index],
            device_id={"cls": near["x+"]},
        ).wait_recv()
        begin(kind, u, v, outs)
    lax.fori_loop(1, N_CLS, wait_small, 0)
    own.wait()
    small_own.wait()
    for copy in sent:
        copy.wait_send()


def gather_images(embeddings, small):
    rows, width = embeddings.shape
    parts = len(relay_order(rows)[1])
    return pl.pallas_call(
        gather_kernel,
        out_shape=[
            jax.ShapeDtypeStruct((N_CLS, rows, width), embeddings.dtype),
            jax.ShapeDtypeStruct((N_CLS,) + small.shape, small.dtype),
        ],
        in_specs=[pl.BlockSpec(memory_space=pltpu.VMEM), pl.BlockSpec(memory_space=pltpu.VMEM)],
        out_specs=[pl.BlockSpec(memory_space=pltpu.HBM), pl.BlockSpec(memory_space=pltpu.VMEM)],
        scratch_shapes=[
            pltpu.SemaphoreType.DMA((parts,)),
            pltpu.SemaphoreType.DMA((parts,)),
            pltpu.SemaphoreType.DMA((2,)),
            pltpu.SemaphoreType.DMA((N_CLS,)),
            pltpu.SemaphoreType.DMA((N_CLS,)),
        ],
        compiler_params=pltpu.CompilerParams(collective_id=1, has_side_effects=True),
        name="gather_images",
    )(embeddings, small)


def scatter_kernel(grad_ref, out_ref, pair, arrived, held, send_p, recv_p, send_r, recv_r):
    dp = lax.axis_index("dp")
    z, core = dp // 2, dp % 2
    other = z * 2 + (1 - core)
    up, down = ((z + 1) % NZ) * 2 + core, ((z + NZ - 1) % NZ) * 2 + core
    barrier = pltpu.get_barrier_semaphore()
    for target in (other, up, down):
        pl.semaphore_signal(barrier, inc=1, device_id={"dp": target})
    pl.semaphore_wait(barrier, 3)
    chains = grad_ref.shape[0]

    def chunk_of(chain, step):
        if chain < chains // 2:
            return (z + NZ - 1 - step) % NZ
        return (z + 1 + step) % NZ

    def pair_copy(chain, step):
        return pltpu.make_async_remote_copy(
            src_ref=grad_ref.at[chain, chunk_of(chain, step) * 2 + (1 - core)],
            dst_ref=pair.at[chain, step],
            send_sem=send_p.at[chain, step],
            recv_sem=recv_p.at[chain, step],
            device_id={"dp": other},
        )

    def ring_copy(chain, step):
        return pltpu.make_async_remote_copy(
            src_ref=held.at[chain, step],
            dst_ref=arrived.at[chain, step],
            send_sem=send_r.at[chain, step],
            recv_sem=recv_r.at[chain, step],
            device_id={"dp": up if chain < chains // 2 else down},
        )

    order = [0, chains // 2, 1, chains // 2 + 1]
    for step in range(NZ):
        for chain in order:
            pair_copy(chain, step).start()
    for step in range(NZ):
        for chain in order:
            pair_copy(chain, step).wait_recv()
            value = grad_ref[chain, chunk_of(chain, step) * 2 + core] + pair[chain, step]
            if step > 0:
                ring_copy(chain, step - 1).wait_recv()
                value = value + arrived[chain, step - 1]
            if step < NZ - 1:
                held[chain, step] = value
                ring_copy(chain, step).start()
            else:
                out_ref[chain] = value
    for step in range(NZ):
        for chain in order:
            pair_copy(chain, step).wait_send()
            if step < NZ - 1:
                ring_copy(chain, step).wait_send()


def scatter_grad(grad):
    chains, shares, rows, width = grad.shape
    return pl.pallas_call(
        scatter_kernel,
        out_shape=jax.ShapeDtypeStruct((chains, rows, width), jnp.float32),
        in_specs=[pl.BlockSpec(memory_space=pltpu.VMEM)],
        out_specs=pl.BlockSpec(memory_space=pltpu.VMEM),
        scratch_shapes=[
            pltpu.VMEM((chains, NZ, rows, width), jnp.float32),
            pltpu.VMEM((chains, NZ, rows, width), jnp.float32),
            pltpu.VMEM((chains, NZ, rows, width), jnp.float32),
            pltpu.SemaphoreType.DMA((chains, NZ)),
            pltpu.SemaphoreType.DMA((chains, NZ)),
            pltpu.SemaphoreType.DMA((chains, NZ)),
            pltpu.SemaphoreType.DMA((chains, NZ)),
        ],
        compiler_params=pltpu.CompilerParams(collective_id=2, has_side_effects=True),
        name="scatter_grad",
    )(grad)


def body(embeddings, class_rows, cand_blocks, label_pos):
    local_blocks, block_taxa, feature_width = class_rows.shape
    own_images, (own_lists, listed) = label_pos.shape[0], cand_blocks.shape
    small = jnp.concatenate([label_pos, cand_blocks.reshape(-1)])
    small = jnp.pad(small, (0, 8 * 128 - small.shape[0])).reshape(8, 128)
    gathered, small_all = gather_images(embeddings, small)
    gathered = gathered.reshape(N_CLS * own_images, feature_width)
    small_all = small_all.reshape(N_CLS, 8 * 128)
    labels_all = small_all[:, :own_images].reshape(-1)
    cand_all = small_all[:, own_images : own_images + own_lists * listed].reshape(-1, listed)
    group_lists = cand_all.shape[0]
    dp_images = gathered.shape[0]
    group_rows = dp_images // group_lists
    my_shard = lax.axis_index("cls")
    owned_ids = my_shard * local_blocks + jnp.arange(local_blocks, dtype=jnp.int32)
    matches = (cand_all[:, :, None] == owned_ids[None, None, :]).astype(jnp.int32)
    hit_count = jnp.sum(matches, axis=1)
    slot_of = jnp.sum(
        matches * jnp.arange(cand_all.shape[1], dtype=jnp.int32)[None, :, None], axis=1
    )
    hit_rank = jnp.cumsum(hit_count, axis=0) - 1
    slot_ids = jnp.arange(MOST, dtype=jnp.int32)
    picked = (
        (hit_count[:, :, None] > 0) & (hit_rank[:, :, None] == slot_ids[None, None, :])
    ).astype(jnp.int32)
    block_index = jnp.arange(group_lists, dtype=jnp.int32)[:, None, None]
    src_block = jnp.sum(picked * block_index, axis=0)
    valid_slot = jnp.sum(picked, axis=0)
    src_slot = jnp.sum(picked * slot_of[:, :, None], axis=0)
    image_tiles = gathered.reshape(group_lists, group_rows, feature_width)[src_block]
    label_tiles = labels_all.reshape(group_lists, group_rows)[src_block]
    scores = jnp.einsum(
        "jsid,jtd->jsit", image_tiles, class_rows, preferred_element_type=jnp.float32
    )
    live_slot = (valid_slot > 0)[:, :, None, None]
    target_pos = (
        src_slot[:, :, None, None] * block_taxa
        + jnp.arange(block_taxa, dtype=jnp.int32)[None, None, None, :]
    )
    is_true = (label_tiles[:, :, :, None] == target_pos) & live_slot
    slot_true = jnp.sum(jnp.where(is_true, scores, 0.0), axis=3)
    slot_max = jnp.max(scores, axis=3)
    slot_sum = jnp.sum(jnp.exp(scores - slot_max[..., None]), axis=3)
    owner_map = picked.reshape(group_lists, local_blocks * MOST)
    owner_float = owner_map.astype(jnp.float32)
    flat_max = slot_max.reshape(local_blocks * MOST, group_rows)
    local_max = jnp.max(jnp.where(owner_map[:, :, None] > 0, flat_max[None, :, :], NEG), axis=1)
    base = local_max[src_block.reshape(-1)]
    scaled = jnp.where(
        valid_slot.reshape(-1, 1) > 0,
        jnp.exp(flat_max - base) * slot_sum.reshape(-1, group_rows),
        0.0,
    )
    sums = jnp.einsum(
        "bq,qi->bi",
        owner_float,
        jnp.concatenate([scaled, slot_true.reshape(-1, group_rows)], axis=1),
        precision=lax.Precision.HIGHEST,
    )
    local_sum, local_true = sums[:, :group_rows], sums[:, group_rows:]
    per = group_lists // N_CLS
    parts = [a.reshape(N_CLS, per, group_rows) for a in (local_max, local_sum, local_true)]
    parts.append(jnp.zeros((N_CLS, 8 - 3 * per, group_rows), jnp.float32))
    combined = combine_stats(jnp.concatenate(parts, axis=1))
    log_norm = combined[:, 0:per].reshape(group_lists, group_rows)
    image_loss = combined[:, per : 2 * per].reshape(dp_images)
    softmax_prob = jnp.exp(scores - log_norm[src_block][:, :, :, None])
    logit_grad = jnp.where(live_slot, softmax_prob - is_true.astype(jnp.float32), 0.0).astype(
        jnp.bfloat16
    )
    grad = jnp.einsum(
        "jsit,jsid->jtd", logit_grad, image_tiles, preferred_element_type=jnp.float32
    )
    shares = lax.axis_size("dp")
    grad = grad.reshape(local_blocks, shares, block_taxa // shares, feature_width)
    class_grad = scatter_grad(grad).transpose(1, 0, 2)
    return (image_loss, class_grad)


def solution(mesh):
    in_specs = (
        P(("dp", "cls"), None),
        P("cls", None, None),
        P(("dp", "cls"), None),
        P(("dp", "cls")),
    )
    out_specs = (P("dp"), P("dp", "cls", None))
    return jax.shard_map(body, mesh=mesh, in_specs=in_specs, out_specs=out_specs, check_vma=False)
```

```python
import jax
import jax.numpy as jnp
from jax import lax
from jax.experimental import pallas as pl
from jax.experimental.pallas import tpu as pltpu
from jax.sharding import PartitionSpec as P

MOST = 8
NEG = -3.0e38
N_CLS = 32


NX, NY, NZ = 4, 8, 8
A_ROWS = 96
BLOCKS = 4


def relay_order(rows):
    rate = 30.0
    hop = 1.7
    a_rows, b_rows = A_ROWS, rows - A_ROWS
    free = {"x+": 0.0, "x-": 0.0, "y+": 0.0, "y-": 0.0}
    queue, serial, order = [], 0, []

    def span(kind, u, v):
        size, start = (a_rows, 0) if kind == "A" else (b_rows, a_rows)
        first, second = (u, v) if kind == "A" else (v, u)
        far1, far2 = (NX // 2, NY // 2) if kind == "A" else (NY // 2, NX // 2)
        if abs(first) == far1:
            return (start, size // 2) if first < 0 else (start + size // 2, size // 2)
        if abs(second) == far2:
            return (start, size // 2) if second < 0 else (start + size // 2, size // 2)
        return start, size

    def sends(kind, u, v, came):
        result = []
        first_axis = "x" if kind == "A" else "y"
        for axis in ("x", "y"):
            pos, far = (u, NX // 2) if axis == "x" else (v, NY // 2)
            if axis == first_axis and came is not None and came[0] != first_axis:
                continue
            for sign in ("+", "-"):
                if came is not None and came[0] == axis and came[1] != sign:
                    continue
                new = pos - 1 if sign == "+" else pos + 1
                if abs(new) > far:
                    continue
                if axis != first_axis and abs(new) == far:
                    first, far1 = (u, NX // 2) if kind == "A" else (v, NY // 2)
                    if abs(first) == far1 and (first < 0) != (new < 0):
                        continue
                result.append((axis + sign, (new, v) if axis == "x" else (u, new)))
        result.sort(key=lambda item: item[0][0] != first_axis)
        return result

    def launch(now, kind, u, v, came):
        nonlocal serial
        out = []
        for direction, (nu, nv) in sends(kind, u, v, came):
            start, size = span(kind, nu, nv)
            free[direction] = max(free[direction], now) + size / rate
            queue.append((free[direction] + hop, serial, kind, nu, nv, direction))
            serial += 1
            out.append((direction, nu, nv, start, size))
        return out

    first = [("A", launch(0.0, "A", 0, 0, None)), ("B", launch(0.0, "B", 0, 0, None))]
    while queue:
        queue.sort()
        now, _, kind, u, v, direction = queue.pop(0)
        start, size = span(kind, u, v)
        order.append((kind, u, v, start, size, launch(now, kind, u, v, direction)))
    return first, order


def gather_kernel(own_ref, small_ref, out_ref, small_out, send, recv, local, small_send, small_recv):
    me = lax.axis_index("cls")
    x, y = me // NY, me % NY
    barrier = pltpu.get_barrier_semaphore()

    def greet(step, carry):
        pl.semaphore_signal(barrier, inc=1, device_id={"cls": (me + step) % N_CLS})
        return carry

    lax.fori_loop(1, N_CLS, greet, 0)
    pl.semaphore_wait(barrier, N_CLS - 1)

    rows = own_ref.shape[0]
    first, order = relay_order(rows)
    near = {
        "x+": ((x + 1) % NX) * NY + y,
        "x-": ((x + NX - 1) % NX) * NY + y,
        "y+": x * NY + (y + 1) % NY,
        "y-": x * NY + (y + NY - 1) % NY,
    }
    number = {(kind, u, v): i for i, (kind, u, v, _, _, _) in enumerate(order)}
    sent = []

    def slot_of(u, v):
        return ((x + u + NX) % NX) * NY + (y + v + NY) % NY

    def begin(kind, u, v, outs):
        slot = slot_of(u, v)
        for direction, nu, nv, start, size in outs:
            index = number[(kind, nu, nv)]
            source = own_ref if (u, v) == (0, 0) else out_ref.at[slot]
            copy = pltpu.make_async_remote_copy(
                src_ref=source.at[pl.ds(start, size)],
                dst_ref=out_ref.at[slot, pl.ds(start, size)],
                send_sem=send.at[index],
                recv_sem=recv.at[index],
                device_id={"cls": near[direction]},
            )
            copy.start()
            sent.append(copy)

    def small_copy(step):
        return pltpu.make_async_remote_copy(
            src_ref=small_ref,
            dst_ref=small_out.at[me],
            send_sem=small_send.at[step],
            recv_sem=small_recv.at[step],
            device_id={"cls": (me + step) % N_CLS},
        )

    def start_small(step, carry):
        small_copy(step).start()
        return carry

    def wait_small(step, carry):
        small_copy(step).wait()
        return carry

    for kind, outs in first:
        begin(kind, 0, 0, outs)
    lax.fori_loop(1, N_CLS, start_small, 0)
    own = pltpu.make_async_copy(own_ref, out_ref.at[me], local.at[0])
    own.start()
    small_own = pltpu.make_async_copy(small_ref, small_out.at[me], local.at[1])
    small_own.start()
    for index, (kind, u, v, start, size, outs) in enumerate(order):
        pltpu.make_async_remote_copy(
            src_ref=own_ref.at[pl.ds(start, size)],
            dst_ref=out_ref.at[slot_of(u, v), pl.ds(start, size)],
            send_sem=send.at[index],
            recv_sem=recv.at[index],
            device_id={"cls": near["x+"]},
        ).wait_recv()
        begin(kind, u, v, outs)
    lax.fori_loop(1, N_CLS, wait_small, 0)
    own.wait()
    small_own.wait()
    for copy in sent:
        copy.wait_send()


def gather_images(embeddings, small):
    rows, width = embeddings.shape
    parts = len(relay_order(rows)[1])
    return pl.pallas_call(
        gather_kernel,
        out_shape=[
            jax.ShapeDtypeStruct((N_CLS, rows, width), embeddings.dtype),
            jax.ShapeDtypeStruct((N_CLS,) + small.shape, small.dtype),
        ],
        in_specs=[pl.BlockSpec(memory_space=pltpu.VMEM), pl.BlockSpec(memory_space=pltpu.VMEM)],
        out_specs=[pl.BlockSpec(memory_space=pltpu.HBM), pl.BlockSpec(memory_space=pltpu.VMEM)],
        scratch_shapes=[
            pltpu.SemaphoreType.DMA((parts,)),
            pltpu.SemaphoreType.DMA((parts,)),
            pltpu.SemaphoreType.DMA((2,)),
            pltpu.SemaphoreType.DMA((N_CLS,)),
            pltpu.SemaphoreType.DMA((N_CLS,)),
        ],
        compiler_params=pltpu.CompilerParams(collective_id=1, has_side_effects=True),
        name="gather_images",
    )(embeddings, small)


def score_kernel(src_ref, one_ref, two_ref, rows_ref, target_ref, pick_ref, scores_ref, picked_ref, stats_ref, slot_stats):
    del src_ref
    p = pl.program_id(0)
    picked_ref[0] = one_ref[0]
    picked_ref[1] = two_ref[0]
    both = jnp.concatenate([one_ref[0], two_ref[0]], axis=0)
    score = lax.dot_general(
        rows_ref[0], both, (((1,), (1,)), ((), ())), preferred_element_type=jnp.float32
    )
    taxon = lax.broadcasted_iota(jnp.int32, (256, 128), 0)
    for i in range(2):
        part = score[:, i * 128 : (i + 1) * 128]
        scores_ref[i] = part
        top = jnp.max(part, axis=0, keepdims=True)
        q = 2 * p + i
        slot_stats[q, 0:1, :] = top
        slot_stats[q, 1:2, :] = jnp.sum(jnp.exp(part - top), axis=0, keepdims=True)
        slot_stats[q, 2:3, :] = jnp.sum(
            jnp.where(taxon == target_ref[i], part, 0.0), axis=0, keepdims=True
        )

    @pl.when(p == BLOCKS * MOST // 2 - 1)
    def merge():
        list_of = lax.broadcasted_iota(jnp.int32, (2 * N_CLS, 128), 0)

        def merge_top(q, top):
            return jnp.where(list_of == pick_ref[q], jnp.maximum(top, slot_stats[q, 0:1, :]), top)

        local_top = lax.fori_loop(
            0, BLOCKS * MOST, merge_top, jnp.full((2 * N_CLS, 128), NEG, jnp.float32), unroll=4
        )

        def merge_sum(q, carry):
            total, true_score = carry
            sel = list_of == pick_ref[q]
            scaled = jnp.exp(slot_stats[q, 0:1, :] - local_top) * slot_stats[q, 1:2, :]
            return (
                total + jnp.where(sel, scaled, 0.0),
                true_score + jnp.where(sel, slot_stats[q, 2:3, :], 0.0),
            )

        zero = jnp.zeros((2 * N_CLS, 128), jnp.float32)
        local_sum, local_true = lax.fori_loop(0, BLOCKS * MOST, merge_sum, (zero, zero), unroll=4)
        for d in range(N_CLS):
            for i, array in enumerate((local_top, local_sum, local_true)):
                stats_ref[d, 2 * i : 2 * i + 2, :] = array[2 * d : 2 * d + 2, :]
            stats_ref[d, 6:8, :] = jnp.zeros((2, 128), jnp.float32)


def score_slots(src, images, class_rows, target, pick):
    slots = BLOCKS * MOST
    _, taxa, width = class_rows.shape
    return pl.pallas_call(
        score_kernel,
        grid_spec=pltpu.PrefetchScalarGridSpec(
            num_scalar_prefetch=1,
            grid=(slots // 2,),
            in_specs=[
                pl.BlockSpec((1, 128, width), lambda p, src: (src[2 * p], 0, 0)),
                pl.BlockSpec((1, 128, width), lambda p, src: (src[2 * p + 1], 0, 0)),
                pl.BlockSpec((1, taxa, width), lambda p, src: (p // (MOST // 2), 0, 0)),
                pl.BlockSpec((2, 1, 128), lambda p, src: (p, 0, 0)),
                pl.BlockSpec((slots, 1, 128), lambda p, src: (0, 0, 0)),
            ],
            out_specs=[
                pl.BlockSpec((2, taxa, 128), lambda p, src: (p, 0, 0)),
                pl.BlockSpec((2, 128, width), lambda p, src: (p, 0, 0)),
                pl.BlockSpec((N_CLS, 8, 128), lambda p, src: (0, 0, 0)),
            ],
            scratch_shapes=[pltpu.VMEM((slots, 8, 128), jnp.float32)],
        ),
        out_shape=[
            jax.ShapeDtypeStruct((slots, taxa, 128), jnp.float32),
            jax.ShapeDtypeStruct((slots, 128, width), jnp.bfloat16),
            jax.ShapeDtypeStruct((N_CLS, 8, 128), jnp.float32),
        ],
        name="score_slots",
    )(src, images, images, class_rows, target, pick)


def grad_kernel(
    stats, target_ref, pick_ref, scores_in, picked_in, lse_ref, out_ref,
    scores, picked, recv, mine, probs, grad, pair, arrived, held,
    send_a, recv_a, send_b, recv_b, send_p, recv_p, send_r, recv_r, local,
):
    me = lax.axis_index("cls")
    dp = lax.axis_index("dp")
    z, core = dp // 2, dp % 2
    other = z * 2 + (1 - core)
    up, down = ((z + 1) % NZ) * 2 + core, ((z + NZ - 1) % NZ) * 2 + core
    barrier = pltpu.get_barrier_semaphore()

    def greet(step, carry):
        pl.semaphore_signal(barrier, inc=1, device_id={"cls": (me + step) % N_CLS})
        return carry

    lax.fori_loop(1, N_CLS, greet, 0)
    for target in (other, up, down):
        pl.semaphore_signal(barrier, inc=1, device_id={"dp": target})
    take_scores = pltpu.make_async_copy(scores_in, scores, local.at[0])
    take_picked = pltpu.make_async_copy(picked_in, picked, local.at[1])
    take_scores.start()
    take_picked.start()
    pl.semaphore_wait(barrier, N_CLS + 2)

    def part_copy(step):
        target = (me + step) % N_CLS
        return pltpu.make_async_remote_copy(
            src_ref=stats.at[target],
            dst_ref=recv.at[step],
            send_sem=send_a.at[step],
            recv_sem=recv_a.at[step],
            device_id={"cls": target},
        )

    def start_part(step, carry):
        part_copy(step).start()
        return carry

    def wait_part(step, carry):
        part_copy(step).wait()
        return carry

    lax.fori_loop(1, N_CLS, start_part, 0)
    recv[0] = stats[me]
    lax.fori_loop(1, N_CLS, wait_part, 0)

    parts = recv[...]
    tops = parts[:, 0:2, :]
    top = jnp.max(tops, axis=0)
    total = jnp.sum(jnp.exp(tops - top[None]) * parts[:, 2:4, :], axis=0)
    true_score = jnp.sum(parts[:, 4:6, :], axis=0)
    log_norm = top + jnp.log(total)
    mine[0:2, :] = log_norm
    mine[2:4, :] = log_norm - true_score
    mine[4:8, :] = jnp.zeros((4, 128), jnp.float32)
    lse_ref[me] = mine[...]

    def whole_copy(step):
        return pltpu.make_async_remote_copy(
            src_ref=mine,
            dst_ref=lse_ref.at[me],
            send_sem=send_b.at[step],
            recv_sem=recv_b.at[step],
            device_id={"cls": (me + step) % N_CLS},
        )

    def start_whole(step, carry):
        whole_copy(step).start()
        return carry

    def wait_whole(step, carry):
        whole_copy(step).wait()
        return carry

    lax.fori_loop(1, N_CLS, start_whole, 0)
    lax.fori_loop(1, N_CLS, wait_whole, 0)

    norms = jnp.concatenate([lse_ref[d, 0:2, :] for d in range(N_CLS)], axis=0)
    list_of = lax.broadcasted_iota(jnp.int32, (2 * N_CLS, 128), 0)
    taxon = lax.broadcasted_iota(jnp.int32, (256, 128), 0)
    take_scores.wait()
    take_picked.wait()

    def chunk_of(chain, step):
        if chain < BLOCKS // 2:
            return (z + NZ - 1 - step) % NZ
        return (z + 1 + step) % NZ

    def pair_copy(chain, step):
        return pltpu.make_async_remote_copy(
            src_ref=grad.at[chain, chunk_of(chain, step) * 2 + (1 - core)],
            dst_ref=pair.at[chain, step],
            send_sem=send_p.at[chain, step],
            recv_sem=recv_p.at[chain, step],
            device_id={"dp": other},
        )

    def ring_copy(chain, half, step):
        return pltpu.make_async_remote_copy(
            src_ref=held.at[chain, step, half],
            dst_ref=arrived.at[chain, step, half],
            send_sem=send_r.at[chain, step, half],
            recv_sem=recv_r.at[chain, step, half],
            device_id={"dp": up if chain < BLOCKS // 2 else down},
        )

    turn = [0, BLOCKS // 2, 1, BLOCKS // 2 + 1]
    for j in turn:
        for s in range(MOST):
            q = j * MOST + s
            pick = pick_ref[q]
            norm = jnp.sum(jnp.where(list_of == pick, norms, 0.0), axis=0, keepdims=True)
            prob = jnp.exp(scores[q] - norm)
            hot = (taxon == target_ref[q]).astype(jnp.float32)
            value = jnp.where(taxon + pick >= taxon, prob - hot, 0.0)
            probs[:, s * 128 : (s + 1) * 128] = value.astype(jnp.bfloat16)
        total = jnp.dot(
            probs[...],
            picked[j * MOST : (j + 1) * MOST].reshape(MOST * 128, picked.shape[2]),
            preferred_element_type=jnp.float32,
        )
        grad[j] = total.reshape(grad.shape[1:])
        for step in range(NZ):
            pair_copy(j, step).start()
    for step in range(NZ):
        for chain in turn:
            pair_copy(chain, step).wait_recv()
            for half in range(2):
                span = pl.ds(half * 8, 8)
                value = (
                    grad[chain, chunk_of(chain, step) * 2 + core, span, :]
                    + pair[chain, step, span, :]
                )
                if step > 0:
                    ring_copy(chain, half, step - 1).wait_recv()
                    value = value + arrived[chain, step - 1, half]
                if step < NZ - 1:
                    held[chain, step, half] = value
                    ring_copy(chain, half, step).start()
                else:
                    out_ref[chain, span, :] = value
    for step in range(NZ):
        for chain in turn:
            pair_copy(chain, step).wait_send()
            if step < NZ - 1:
                for half in range(2):
                    ring_copy(chain, half, step).wait_send()


def combine_and_scatter(stats, target, pick, scores, picked, shares):
    slots, taxa, _ = scores.shape
    width, share = picked.shape[2], taxa // shares
    vmem = pl.BlockSpec(memory_space=pltpu.VMEM)
    hbm = pl.BlockSpec(memory_space=pltpu.HBM)
    dma = pltpu.SemaphoreType.DMA
    return pl.pallas_call(
        grad_kernel,
        out_shape=[
            jax.ShapeDtypeStruct((N_CLS, 8, 128), jnp.float32),
            jax.ShapeDtypeStruct((BLOCKS, share, width), jnp.float32),
        ],
        in_specs=[vmem] * 3 + [hbm] * 2,
        out_specs=[vmem] * 2,
        scratch_shapes=[
            pltpu.VMEM((slots, taxa, 128), jnp.float32),
            pltpu.VMEM((slots, 128, width), jnp.bfloat16),
            pltpu.VMEM((N_CLS, 8, 128), jnp.float32),
            pltpu.VMEM((8, 128), jnp.float32),
            pltpu.VMEM((taxa, MOST * 128), jnp.bfloat16),
            pltpu.VMEM((BLOCKS, shares, share, width), jnp.float32),
            pltpu.VMEM((BLOCKS, NZ, share, width), jnp.float32),
            pltpu.VMEM((BLOCKS, NZ, 2, share // 2, width), jnp.float32),
            pltpu.VMEM((BLOCKS, NZ, 2, share // 2, width), jnp.float32),
            dma((N_CLS,)),
            dma((N_CLS,)),
            dma((N_CLS,)),
            dma((N_CLS,)),
            dma((BLOCKS, NZ)),
            dma((BLOCKS, NZ)),
            dma((BLOCKS, NZ, 2)),
            dma((BLOCKS, NZ, 2)),
            dma((2,)),
        ],
        compiler_params=pltpu.CompilerParams(
            collective_id=0, has_side_effects=True, vmem_limit_bytes=48 * 1024 * 1024
        ),
        name="combine_and_scatter",
    )(stats, target, pick, scores, picked)


def body(embeddings, class_rows, cand_blocks, label_pos):
    local_blocks, block_taxa, feature_width = class_rows.shape
    own_images, (own_lists, listed) = label_pos.shape[0], cand_blocks.shape
    small = jnp.concatenate([label_pos, cand_blocks.reshape(-1)])
    small = jnp.pad(small, (0, 8 * 128 - small.shape[0])).reshape(8, 128)
    gathered, small_all = gather_images(embeddings, small)
    gathered = gathered.reshape(N_CLS * own_images, feature_width)
    small_all = small_all.reshape(N_CLS, 8 * 128)
    labels_all = small_all[:, :own_images].reshape(-1)
    cand_all = small_all[:, own_images : own_images + own_lists * listed].reshape(-1, listed)
    group_lists = cand_all.shape[0]
    dp_images = gathered.shape[0]
    group_rows = dp_images // group_lists
    my_shard = lax.axis_index("cls")
    owned_ids = my_shard * local_blocks + jnp.arange(local_blocks, dtype=jnp.int32)
    matches = (cand_all[:, :, None] == owned_ids[None, None, :]).astype(jnp.int32)
    hit_count = jnp.sum(matches, axis=1)
    slot_of = jnp.sum(
        matches * jnp.arange(cand_all.shape[1], dtype=jnp.int32)[None, :, None], axis=1
    )
    hit_rank = jnp.cumsum(hit_count, axis=0) - 1
    slot_ids = jnp.arange(MOST, dtype=jnp.int32)
    chosen = (
        (hit_count[:, :, None] > 0) & (hit_rank[:, :, None] == slot_ids[None, None, :])
    ).astype(jnp.int32)
    block_index = jnp.arange(group_lists, dtype=jnp.int32)[:, None, None]
    src_block = jnp.sum(chosen * block_index, axis=0)
    valid_slot = jnp.sum(chosen, axis=0)
    src_slot = jnp.sum(chosen * slot_of[:, :, None], axis=0)
    valid = valid_slot.reshape(-1, 1) > 0
    label_tiles = labels_all.reshape(group_lists, group_rows)[src_block.reshape(-1)]
    target = jnp.where(valid, label_tiles - src_slot.reshape(-1, 1) * block_taxa, -1)
    pick = jnp.broadcast_to(jnp.where(valid, src_block.reshape(-1, 1), -1), target.shape)
    target, pick = target[:, None, :], pick[:, None, :]
    scores, picked, stats = score_slots(
        src_block.reshape(-1), gathered.reshape(group_lists, group_rows, feature_width), class_rows, target, pick
    )
    combined, grad = combine_and_scatter(stats, target, pick, scores, picked, lax.axis_size("dp"))
    per = group_lists // N_CLS
    image_loss = combined[:, per : 2 * per].reshape(dp_images)
    class_grad = grad.transpose(1, 0, 2)
    return (image_loss, class_grad)


def solution(mesh):
    in_specs = (
        P(("dp", "cls"), None),
        P("cls", None, None),
        P(("dp", "cls"), None),
        P(("dp", "cls")),
    )
    out_specs = (P("dp"), P("dp", "cls", None))
    return jax.shard_map(body, mesh=mesh, in_specs=in_specs, out_specs=out_specs, check_vma=False)
```

```python
import jax
import jax.numpy as jnp
from jax import lax
from jax.experimental import pallas as pl
from jax.experimental.pallas import tpu as pltpu
from jax.sharding import PartitionSpec as P

MOST = 8
NEG = -3.0e38
N_CLS = 32


NX, NY, NZ = 4, 8, 8
A_ROWS = 104
BLOCKS = 4


def relay_order(rows):
    rate = 30.0
    hop = 1.7
    a_rows, b_rows = A_ROWS, rows - A_ROWS
    free = {"x+": 0.0, "x-": 0.0, "y+": 0.0, "y-": 0.0}
    queue, serial, order = [], 0, []

    def span(kind, u, v):
        size, start = (a_rows, 0) if kind == "A" else (b_rows, a_rows)
        first, second = (u, v) if kind == "A" else (v, u)
        far1, far2 = (NX // 2, NY // 2) if kind == "A" else (NY // 2, NX // 2)
        if abs(first) == far1 or abs(second) == far2:
            before = first if abs(first) == far1 else second
            lower = -(-size // 16) * 8
            return (start, lower) if before < 0 else (start + lower, size - lower)
        return start, size

    def sends(kind, u, v, came):
        result = []
        first_axis = "x" if kind == "A" else "y"
        for axis in ("x", "y"):
            pos, far = (u, NX // 2) if axis == "x" else (v, NY // 2)
            if axis == first_axis and came is not None and came[0] != first_axis:
                continue
            for sign in ("+", "-"):
                if came is not None and came[0] == axis and came[1] != sign:
                    continue
                new = pos - 1 if sign == "+" else pos + 1
                if abs(new) > far:
                    continue
                if axis != first_axis and abs(new) == far:
                    first, far1 = (u, NX // 2) if kind == "A" else (v, NY // 2)
                    if abs(first) == far1 and (first < 0) != (new < 0):
                        continue
                result.append((axis + sign, (new, v) if axis == "x" else (u, new)))
        result.sort(key=lambda item: item[0][0] != first_axis)
        return result

    def launch(now, kind, u, v, came):
        nonlocal serial
        out = []
        for direction, (nu, nv) in sends(kind, u, v, came):
            start, size = span(kind, nu, nv)
            free[direction] = max(free[direction], now) + size / rate
            queue.append((free[direction] + hop, serial, kind, nu, nv, direction))
            serial += 1
            out.append((direction, nu, nv, start, size))
        return out

    first = [("A", launch(0.0, "A", 0, 0, None)), ("B", launch(0.0, "B", 0, 0, None))]
    while queue:
        queue.sort()
        now, _, kind, u, v, direction = queue.pop(0)
        start, size = span(kind, u, v)
        order.append((kind, u, v, start, size, launch(now, kind, u, v, direction)))
    return first, order


def gather_kernel(own_ref, small_ref, out_ref, small_out, send, recv, local, small_send, small_recv):
    me = lax.axis_index("cls")
    x, y = me // NY, me % NY
    barrier = pltpu.get_barrier_semaphore()

    def greet(step, carry):
        pl.semaphore_signal(barrier, inc=1, device_id={"cls": (me + step) % N_CLS})
        return carry

    lax.fori_loop(1, N_CLS, greet, 0)
    pl.semaphore_wait(barrier, N_CLS - 1)

    rows = own_ref.shape[0]
    first, order = relay_order(rows)
    near = {
        "x+": ((x + 1) % NX) * NY + y,
        "x-": ((x + NX - 1) % NX) * NY + y,
        "y+": x * NY + (y + 1) % NY,
        "y-": x * NY + (y + NY - 1) % NY,
    }
    number = {(kind, u, v): i for i, (kind, u, v, _, _, _) in enumerate(order)}
    sent = []

    def slot_of(u, v):
        return ((x + u + NX) % NX) * NY + (y + v + NY) % NY

    def begin(kind, u, v, outs):
        slot = slot_of(u, v)
        for direction, nu, nv, start, size in outs:
            index = number[(kind, nu, nv)]
            source = own_ref if (u, v) == (0, 0) else out_ref.at[slot]
            copy = pltpu.make_async_remote_copy(
                src_ref=source.at[pl.ds(start, size)],
                dst_ref=out_ref.at[slot, pl.ds(start, size)],
                send_sem=send.at[index],
                recv_sem=recv.at[index],
                device_id={"cls": near[direction]},
            )
            copy.start()
            sent.append(copy)

    def small_copy(step):
        return pltpu.make_async_remote_copy(
            src_ref=small_ref,
            dst_ref=small_out.at[me],
            send_sem=small_send.at[step],
            recv_sem=small_recv.at[step],
            device_id={"cls": (me + step) % N_CLS},
        )

    def start_small(step, carry):
        small_copy(step).start()
        return carry

    def wait_small(step, carry):
        small_copy(step).wait()
        return carry

    for kind, outs in first:
        begin(kind, 0, 0, outs)
    lax.fori_loop(1, N_CLS, start_small, 0)
    own = pltpu.make_async_copy(own_ref, out_ref.at[me], local.at[0])
    own.start()
    small_own = pltpu.make_async_copy(small_ref, small_out.at[me], local.at[1])
    small_own.start()
    for index, (kind, u, v, start, size, outs) in enumerate(order):
        pltpu.make_async_remote_copy(
            src_ref=own_ref.at[pl.ds(start, size)],
            dst_ref=out_ref.at[slot_of(u, v), pl.ds(start, size)],
            send_sem=send.at[index],
            recv_sem=recv.at[index],
            device_id={"cls": near["x+"]},
        ).wait_recv()
        begin(kind, u, v, outs)
    lax.fori_loop(1, N_CLS, wait_small, 0)
    own.wait()
    small_own.wait()
    for copy in sent:
        copy.wait_send()


def gather_images(embeddings, small):
    rows, width = embeddings.shape
    parts = len(relay_order(rows)[1])
    return pl.pallas_call(
        gather_kernel,
        out_shape=[
            jax.ShapeDtypeStruct((N_CLS, rows, width), embeddings.dtype),
            jax.ShapeDtypeStruct((N_CLS,) + small.shape, small.dtype),
        ],
        in_specs=[pl.BlockSpec(memory_space=pltpu.VMEM), pl.BlockSpec(memory_space=pltpu.VMEM)],
        out_specs=[pl.BlockSpec(memory_space=pltpu.HBM), pl.BlockSpec(memory_space=pltpu.VMEM)],
        scratch_shapes=[
            pltpu.SemaphoreType.DMA((parts,)),
            pltpu.SemaphoreType.DMA((parts,)),
            pltpu.SemaphoreType.DMA((2,)),
            pltpu.SemaphoreType.DMA((N_CLS,)),
            pltpu.SemaphoreType.DMA((N_CLS,)),
        ],
        compiler_params=pltpu.CompilerParams(collective_id=1, has_side_effects=True),
        name="gather_images",
    )(embeddings, small)


def score_kernel(src_ref, *refs):
    del src_ref
    image_refs = refs[:MOST]
    rows_ref, target_ref, pick_ref, scores_ref, picked_ref, stats_ref, slot_stats = refs[MOST:]
    p = pl.program_id(0)
    taxon = lax.broadcasted_iota(jnp.int32, (256, 128), 0)
    for first in range(0, MOST, 2):
        pair = [image_refs[first][0], image_refs[first + 1][0]]
        picked_ref[first] = pair[0]
        picked_ref[first + 1] = pair[1]
        score = lax.dot_general(
            rows_ref[0],
            jnp.concatenate(pair, axis=0),
            (((1,), (1,)), ((), ())),
            preferred_element_type=jnp.float32,
        )
        for i in range(2):
            part = score[:, i * 128 : (i + 1) * 128]
            scores_ref[first + i] = part
            top = jnp.max(part, axis=0, keepdims=True)
            q = MOST * p + first + i
            slot_stats[q, 0:1, :] = top
            slot_stats[q, 1:2, :] = jnp.sum(jnp.exp(part - top), axis=0, keepdims=True)
            slot_stats[q, 2:3, :] = jnp.sum(
                jnp.where(taxon == target_ref[first + i], part, 0.0), axis=0, keepdims=True
            )

    @pl.when(p == BLOCKS - 1)
    def merge():
        list_of = lax.broadcasted_iota(jnp.int32, (2 * N_CLS, 128), 0)

        def merge_top(q, top):
            return jnp.where(list_of == pick_ref[q], jnp.maximum(top, slot_stats[q, 0:1, :]), top)

        local_top = lax.fori_loop(
            0, BLOCKS * MOST, merge_top, jnp.full((2 * N_CLS, 128), NEG, jnp.float32), unroll=4
        )

        def merge_sum(q, carry):
            total, true_score = carry
            sel = list_of == pick_ref[q]
            scaled = jnp.exp(slot_stats[q, 0:1, :] - local_top) * slot_stats[q, 1:2, :]
            return (
                total + jnp.where(sel, scaled, 0.0),
                true_score + jnp.where(sel, slot_stats[q, 2:3, :], 0.0),
            )

        zero = jnp.zeros((2 * N_CLS, 128), jnp.float32)
        local_sum, local_true = lax.fori_loop(0, BLOCKS * MOST, merge_sum, (zero, zero), unroll=4)
        for d in range(N_CLS):
            for i, array in enumerate((local_top, local_sum, local_true)):
                stats_ref[d, 2 * i : 2 * i + 2, :] = array[2 * d : 2 * d + 2, :]
            stats_ref[d, 6:8, :] = jnp.zeros((2, 128), jnp.float32)


def score_slots(src, images, class_rows, target, pick):
    slots = BLOCKS * MOST
    _, taxa, width = class_rows.shape
    return pl.pallas_call(
        score_kernel,
        grid_spec=pltpu.PrefetchScalarGridSpec(
            num_scalar_prefetch=1,
            grid=(BLOCKS,),
            in_specs=[
                *[
                    pl.BlockSpec((1, 128, width), lambda p, src, i=i: (src[MOST * p + i], 0, 0))
                    for i in range(MOST)
                ],
                pl.BlockSpec((1, taxa, width), lambda p, src: (p, 0, 0)),
                pl.BlockSpec((MOST, 1, 128), lambda p, src: (p, 0, 0)),
                pl.BlockSpec((slots, 1, 128), lambda p, src: (0, 0, 0)),
            ],
            out_specs=[
                pl.BlockSpec((MOST, taxa, 128), lambda p, src: (p, 0, 0)),
                pl.BlockSpec((MOST, 128, width), lambda p, src: (p, 0, 0)),
                pl.BlockSpec((N_CLS, 8, 128), lambda p, src: (0, 0, 0)),
            ],
            scratch_shapes=[pltpu.VMEM((slots, 8, 128), jnp.float32)],
        ),
        out_shape=[
            jax.ShapeDtypeStruct((slots, taxa, 128), jnp.float32),
            jax.ShapeDtypeStruct((slots, 128, width), jnp.bfloat16),
            jax.ShapeDtypeStruct((N_CLS, 8, 128), jnp.float32),
        ],
        name="score_slots",
    )(src, *([images] * MOST), class_rows, target, pick)


def grad_kernel(
    stats, target_ref, pick_ref, scores_in, picked_in, lse_ref, out_ref,
    scores, picked, recv, mine, probs, grad, pair, arrived, held,
    send_a, recv_a, send_b, recv_b, send_p, recv_p, send_r, recv_r, local,
):
    me = lax.axis_index("cls")
    dp = lax.axis_index("dp")
    z, core = dp // 2, dp % 2
    other = z * 2 + (1 - core)
    up, down = ((z + 1) % NZ) * 2 + core, ((z + NZ - 1) % NZ) * 2 + core
    barrier = pltpu.get_barrier_semaphore()

    def greet(step, carry):
        pl.semaphore_signal(barrier, inc=1, device_id={"cls": (me + step) % N_CLS})
        return carry

    lax.fori_loop(1, N_CLS, greet, 0)
    for target in (other, up, down):
        pl.semaphore_signal(barrier, inc=1, device_id={"dp": target})
    take_scores = pltpu.make_async_copy(scores_in, scores, local.at[0])
    take_picked = pltpu.make_async_copy(picked_in, picked, local.at[1])
    take_scores.start()
    take_picked.start()
    pl.semaphore_wait(barrier, N_CLS + 2)

    def part_copy(step):
        target = (me + step) % N_CLS
        return pltpu.make_async_remote_copy(
            src_ref=stats.at[target],
            dst_ref=recv.at[step],
            send_sem=send_a.at[step],
            recv_sem=recv_a.at[step],
            device_id={"cls": target},
        )

    def start_part(step, carry):
        part_copy(step).start()
        return carry

    def wait_part(step, carry):
        part_copy(step).wait()
        return carry

    lax.fori_loop(1, N_CLS, start_part, 0)
    recv[0] = stats[me]
    lax.fori_loop(1, N_CLS, wait_part, 0)

    parts = recv[...]
    tops = parts[:, 0:2, :]
    top = jnp.max(tops, axis=0)
    total = jnp.sum(jnp.exp(tops - top[None]) * parts[:, 2:4, :], axis=0)
    true_score = jnp.sum(parts[:, 4:6, :], axis=0)
    log_norm = top + jnp.log(total)
    mine[0:2, :] = log_norm
    mine[2:4, :] = log_norm - true_score
    mine[4:8, :] = jnp.zeros((4, 128), jnp.float32)
    lse_ref[me] = mine[...]

    def whole_copy(step):
        return pltpu.make_async_remote_copy(
            src_ref=mine,
            dst_ref=lse_ref.at[me],
            send_sem=send_b.at[step],
            recv_sem=recv_b.at[step],
            device_id={"cls": (me + step) % N_CLS},
        )

    def start_whole(step, carry):
        whole_copy(step).start()
        return carry

    def wait_whole(step, carry):
        whole_copy(step).wait()
        return carry

    lax.fori_loop(1, N_CLS, start_whole, 0)
    lax.fori_loop(1, N_CLS, wait_whole, 0)

    norms = jnp.concatenate([lse_ref[d, 0:2, :] for d in range(N_CLS)], axis=0)
    list_of = lax.broadcasted_iota(jnp.int32, (2 * N_CLS, 128), 0)
    taxon = lax.broadcasted_iota(jnp.int32, (256, 128), 0)
    take_scores.wait()
    take_picked.wait()

    def chunk_of(chain, step):
        if chain < BLOCKS // 2:
            return (z + NZ - 1 - step) % NZ
        return (z + 1 + step) % NZ

    def pair_copy(chain, step):
        return pltpu.make_async_remote_copy(
            src_ref=grad.at[chain, chunk_of(chain, step) * 2 + (1 - core)],
            dst_ref=pair.at[chain, step],
            send_sem=send_p.at[chain, step],
            recv_sem=recv_p.at[chain, step],
            device_id={"dp": other},
        )

    def ring_copy(chain, half, step):
        return pltpu.make_async_remote_copy(
            src_ref=held.at[chain, step, half],
            dst_ref=arrived.at[chain, step, half],
            send_sem=send_r.at[chain, step, half],
            recv_sem=recv_r.at[chain, step, half],
            device_id={"dp": up if chain < BLOCKS // 2 else down},
        )

    turn = [0, BLOCKS // 2, 1, BLOCKS // 2 + 1]
    for j in turn:
        for s in range(MOST):
            q = j * MOST + s
            pick = pick_ref[q]
            norm = jnp.sum(jnp.where(list_of == pick, norms, 0.0), axis=0, keepdims=True)
            prob = jnp.exp(scores[q] - norm)
            hot = (taxon == target_ref[q]).astype(jnp.float32)
            value = jnp.where(taxon + pick >= taxon, prob - hot, 0.0)
            probs[:, s * 128 : (s + 1) * 128] = value.astype(jnp.bfloat16)
        total = jnp.dot(
            probs[...],
            picked[j * MOST : (j + 1) * MOST].reshape(MOST * 128, picked.shape[2]),
            preferred_element_type=jnp.float32,
        )
        grad[j] = total.reshape(grad.shape[1:])
        for step in range(NZ):
            pair_copy(j, step).start()
    for step in range(NZ):
        for chain in turn:
            pair_copy(chain, step).wait_recv()
            for half in range(2):
                span = pl.ds(half * 8, 8)
                value = (
                    grad[chain, chunk_of(chain, step) * 2 + core, span, :]
                    + pair[chain, step, span, :]
                )
                if step > 0:
                    ring_copy(chain, half, step - 1).wait_recv()
                    value = value + arrived[chain, step - 1, half]
                if step < NZ - 1:
                    held[chain, step, half] = value
                    ring_copy(chain, half, step).start()
                else:
                    out_ref[chain, span, :] = value
    for step in range(NZ):
        for chain in turn:
            pair_copy(chain, step).wait_send()
            if step < NZ - 1:
                for half in range(2):
                    ring_copy(chain, half, step).wait_send()


def combine_and_scatter(stats, target, pick, scores, picked, shares):
    slots, taxa, _ = scores.shape
    width, share = picked.shape[2], taxa // shares
    vmem = pl.BlockSpec(memory_space=pltpu.VMEM)
    hbm = pl.BlockSpec(memory_space=pltpu.HBM)
    dma = pltpu.SemaphoreType.DMA
    return pl.pallas_call(
        grad_kernel,
        out_shape=[
            jax.ShapeDtypeStruct((N_CLS, 8, 128), jnp.float32),
            jax.ShapeDtypeStruct((BLOCKS, share, width), jnp.float32),
        ],
        in_specs=[vmem] * 3 + [hbm] * 2,
        out_specs=[vmem] * 2,
        scratch_shapes=[
            pltpu.VMEM((slots, taxa, 128), jnp.float32),
            pltpu.VMEM((slots, 128, width), jnp.bfloat16),
            pltpu.VMEM((N_CLS, 8, 128), jnp.float32),
            pltpu.VMEM((8, 128), jnp.float32),
            pltpu.VMEM((taxa, MOST * 128), jnp.bfloat16),
            pltpu.VMEM((BLOCKS, shares, share, width), jnp.float32),
            pltpu.VMEM((BLOCKS, NZ, share, width), jnp.float32),
            pltpu.VMEM((BLOCKS, NZ, 2, share // 2, width), jnp.float32),
            pltpu.VMEM((BLOCKS, NZ, 2, share // 2, width), jnp.float32),
            dma((N_CLS,)),
            dma((N_CLS,)),
            dma((N_CLS,)),
            dma((N_CLS,)),
            dma((BLOCKS, NZ)),
            dma((BLOCKS, NZ)),
            dma((BLOCKS, NZ, 2)),
            dma((BLOCKS, NZ, 2)),
            dma((2,)),
        ],
        compiler_params=pltpu.CompilerParams(
            collective_id=0, has_side_effects=True, vmem_limit_bytes=62 * 1024 * 1024
        ),
        name="combine_and_scatter",
    )(stats, target, pick, scores, picked)


def body(embeddings, class_rows, cand_blocks, label_pos):
    local_blocks, block_taxa, feature_width = class_rows.shape
    own_images, (own_lists, listed) = label_pos.shape[0], cand_blocks.shape
    small = jnp.concatenate([label_pos, cand_blocks.reshape(-1)])
    small = jnp.pad(small, (0, 8 * 128 - small.shape[0])).reshape(8, 128)
    gathered, small_all = gather_images(embeddings, small)
    gathered = gathered.reshape(N_CLS * own_images, feature_width)
    small_all = small_all.reshape(N_CLS, 8 * 128)
    labels_all = small_all[:, :own_images].reshape(-1)
    cand_all = small_all[:, own_images : own_images + own_lists * listed].reshape(-1, listed)
    group_lists = cand_all.shape[0]
    dp_images = gathered.shape[0]
    group_rows = dp_images // group_lists
    my_shard = lax.axis_index("cls")
    owned_ids = my_shard * local_blocks + jnp.arange(local_blocks, dtype=jnp.int32)
    matches = (cand_all[:, :, None] == owned_ids[None, None, :]).astype(jnp.int32)
    hit_count = jnp.sum(matches, axis=1)
    slot_of = jnp.sum(
        matches * jnp.arange(cand_all.shape[1], dtype=jnp.int32)[None, :, None], axis=1
    )
    hit_rank = jnp.cumsum(hit_count, axis=0) - 1
    slot_ids = jnp.arange(MOST, dtype=jnp.int32)
    chosen = (
        (hit_count[:, :, None] > 0) & (hit_rank[:, :, None] == slot_ids[None, None, :])
    ).astype(jnp.int32)
    block_index = jnp.arange(group_lists, dtype=jnp.int32)[:, None, None]
    src_block = jnp.sum(chosen * block_index, axis=0)
    valid_slot = jnp.sum(chosen, axis=0)
    src_slot = jnp.sum(chosen * slot_of[:, :, None], axis=0)
    valid = valid_slot.reshape(-1, 1) > 0
    label_tiles = labels_all.reshape(group_lists, group_rows)[src_block.reshape(-1)]
    target = jnp.where(valid, label_tiles - src_slot.reshape(-1, 1) * block_taxa, -1)
    pick = jnp.broadcast_to(jnp.where(valid, src_block.reshape(-1, 1), -1), target.shape)
    target, pick = target[:, None, :], pick[:, None, :]
    scores, picked, stats = score_slots(
        src_block.reshape(-1), gathered.reshape(group_lists, group_rows, feature_width), class_rows, target, pick
    )
    combined, grad = combine_and_scatter(stats, target, pick, scores, picked, lax.axis_size("dp"))
    per = group_lists // N_CLS
    image_loss = combined[:, per : 2 * per].reshape(dp_images)
    class_grad = grad.transpose(1, 0, 2)
    return (image_loss, class_grad)


def solution(mesh):
    in_specs = (
        P(("dp", "cls"), None),
        P("cls", None, None),
        P(("dp", "cls"), None),
        P(("dp", "cls")),
    )
    out_specs = (P("dp"), P("dp", "cls", None))
    return jax.shard_map(body, mesh=mesh, in_specs=in_specs, out_specs=out_specs, check_vma=False)
```

```python
import jax
import jax.numpy as jnp
from jax import lax
from jax.experimental import pallas as pl
from jax.experimental.pallas import tpu as pltpu
from jax.sharding import PartitionSpec as P

MOST = 8
NEG = -3.0e38
N_CLS = 32


NX, NY, NZ = 4, 8, 8
A_ROWS = 96
BLOCKS = 4


def relay_order(rows):
    rate = 30.0
    hop = 1.7
    a_rows, b_rows = A_ROWS, rows - A_ROWS
    free = {"x+": 0.0, "x-": 0.0, "y+": 0.0, "y-": 0.0}
    queue, serial, order = [], 0, []

    def span(kind, u, v):
        size, start = (a_rows, 0) if kind == "A" else (b_rows, a_rows)
        first, second = (u, v) if kind == "A" else (v, u)
        far1, far2 = (NX // 2, NY // 2) if kind == "A" else (NY // 2, NX // 2)
        if abs(first) == far1 or abs(second) == far2:
            before = first if abs(first) == far1 else second
            lower = -(-size // 16) * 8
            return (start, lower) if before < 0 else (start + lower, size - lower)
        return start, size

    def sends(kind, u, v, came):
        result = []
        first_axis = "x" if kind == "A" else "y"
        for axis in ("x", "y"):
            pos, far = (u, NX // 2) if axis == "x" else (v, NY // 2)
            if axis == first_axis and came is not None and came[0] != first_axis:
                continue
            for sign in ("+", "-"):
                if came is not None and came[0] == axis and came[1] != sign:
                    continue
                new = pos - 1 if sign == "+" else pos + 1
                if abs(new) > far:
                    continue
                if axis != first_axis and abs(new) == far:
                    first, far1 = (u, NX // 2) if kind == "A" else (v, NY // 2)
                    if abs(first) == far1 and (first < 0) != (new < 0):
                        continue
                result.append((axis + sign, (new, v) if axis == "x" else (u, new)))
        result.sort(key=lambda item: item[0][0] != first_axis)
        return result

    def launch(now, kind, u, v, came):
        nonlocal serial
        out = []
        for direction, (nu, nv) in sends(kind, u, v, came):
            start, size = span(kind, nu, nv)
            free[direction] = max(free[direction], now) + size / rate
            queue.append((free[direction] + hop, serial, kind, nu, nv, direction))
            serial += 1
            out.append((direction, nu, nv, start, size))
        return out

    first = [("A", launch(0.0, "A", 0, 0, None)), ("B", launch(0.0, "B", 0, 0, None))]
    while queue:
        queue.sort()
        now, _, kind, u, v, direction = queue.pop(0)
        start, size = span(kind, u, v)
        order.append((kind, u, v, start, size, launch(now, kind, u, v, direction)))
    return first, order


def gather_kernel(own_ref, small_ref, out_ref, small_out, send, recv, local, small_send, small_recv):
    me = lax.axis_index("cls")
    x, y = me // NY, me % NY
    barrier = pltpu.get_barrier_semaphore()

    def greet(step, carry):
        pl.semaphore_signal(barrier, inc=1, device_id={"cls": (me + step) % N_CLS})
        return carry

    lax.fori_loop(1, N_CLS, greet, 0)
    pl.semaphore_wait(barrier, N_CLS - 1)

    rows = own_ref.shape[0]
    first, order = relay_order(rows)
    near = {
        "x+": ((x + 1) % NX) * NY + y,
        "x-": ((x + NX - 1) % NX) * NY + y,
        "y+": x * NY + (y + 1) % NY,
        "y-": x * NY + (y + NY - 1) % NY,
    }
    number = {(kind, u, v): i for i, (kind, u, v, _, _, _) in enumerate(order)}
    sent = []

    def slot_of(u, v):
        return ((x + u + NX) % NX) * NY + (y + v + NY) % NY

    def begin(kind, u, v, outs):
        slot = slot_of(u, v)
        for direction, nu, nv, start, size in outs:
            index = number[(kind, nu, nv)]
            source = own_ref if (u, v) == (0, 0) else out_ref.at[slot]
            copy = pltpu.make_async_remote_copy(
                src_ref=source.at[pl.ds(start, size)],
                dst_ref=out_ref.at[slot, pl.ds(start, size)],
                send_sem=send.at[index],
                recv_sem=recv.at[index],
                device_id={"cls": near[direction]},
            )
            copy.start()
            sent.append(copy)

    def small_copy(step):
        return pltpu.make_async_remote_copy(
            src_ref=small_ref,
            dst_ref=small_out.at[me],
            send_sem=small_send.at[step],
            recv_sem=small_recv.at[step],
            device_id={"cls": (me + step) % N_CLS},
        )

    def start_small(step, carry):
        small_copy(step).start()
        return carry

    def wait_small(step, carry):
        small_copy(step).wait()
        return carry

    for kind, outs in first:
        begin(kind, 0, 0, outs)
    lax.fori_loop(1, N_CLS, start_small, 0)
    own = pltpu.make_async_copy(own_ref, out_ref.at[me], local.at[0])
    own.start()
    small_own = pltpu.make_async_copy(small_ref, small_out.at[me], local.at[1])
    small_own.start()
    for index, (kind, u, v, start, size, outs) in enumerate(order):
        pltpu.make_async_remote_copy(
            src_ref=own_ref.at[pl.ds(start, size)],
            dst_ref=out_ref.at[slot_of(u, v), pl.ds(start, size)],
            send_sem=send.at[index],
            recv_sem=recv.at[index],
            device_id={"cls": near["x+"]},
        ).wait_recv()
        begin(kind, u, v, outs)
    lax.fori_loop(1, N_CLS, wait_small, 0)
    own.wait()
    small_own.wait()
    for copy in sent:
        copy.wait_send()


def gather_images(embeddings, small):
    rows, width = embeddings.shape
    parts = len(relay_order(rows)[1])
    return pl.pallas_call(
        gather_kernel,
        out_shape=[
            jax.ShapeDtypeStruct((N_CLS, rows, width), embeddings.dtype),
            jax.ShapeDtypeStruct((N_CLS,) + small.shape, small.dtype),
        ],
        in_specs=[pl.BlockSpec(memory_space=pltpu.VMEM), pl.BlockSpec(memory_space=pltpu.VMEM)],
        out_specs=[pl.BlockSpec(memory_space=pltpu.HBM), pl.BlockSpec(memory_space=pltpu.VMEM)],
        scratch_shapes=[
            pltpu.SemaphoreType.DMA((parts,)),
            pltpu.SemaphoreType.DMA((parts,)),
            pltpu.SemaphoreType.DMA((2,)),
            pltpu.SemaphoreType.DMA((N_CLS,)),
            pltpu.SemaphoreType.DMA((N_CLS,)),
        ],
        compiler_params=pltpu.CompilerParams(collective_id=1, has_side_effects=True),
        name="gather_images",
    )(embeddings, small)


def score_kernel(src_ref, *refs):
    del src_ref
    image_refs = refs[:MOST]
    rows_ref, target_ref, pick_ref, scores_ref, picked_ref, stats_ref, slot_stats = refs[MOST:]
    p = pl.program_id(0)
    taxon = lax.broadcasted_iota(jnp.int32, (256, 128), 0)
    for first in range(0, MOST, 2):
        pair = [image_refs[first][0], image_refs[first + 1][0]]
        picked_ref[first] = pair[0]
        picked_ref[first + 1] = pair[1]
        score = lax.dot_general(
            rows_ref[0],
            jnp.concatenate(pair, axis=0),
            (((1,), (1,)), ((), ())),
            preferred_element_type=jnp.float32,
        )
        for i in range(2):
            part = score[:, i * 128 : (i + 1) * 128]
            scores_ref[first + i] = part
            top = jnp.max(part, axis=0, keepdims=True)
            q = MOST * p + first + i
            slot_stats[q, 0:1, :] = top
            slot_stats[q, 1:2, :] = jnp.sum(jnp.exp(part - top), axis=0, keepdims=True)
            slot_stats[q, 2:3, :] = jnp.sum(
                jnp.where(taxon == target_ref[first + i], part, 0.0), axis=0, keepdims=True
            )

    @pl.when(p == BLOCKS - 1)
    def merge():
        list_of = lax.broadcasted_iota(jnp.int32, (2 * N_CLS, 128), 0)

        def merge_top(q, top):
            return jnp.where(list_of == pick_ref[q], jnp.maximum(top, slot_stats[q, 0:1, :]), top)

        local_top = lax.fori_loop(
            0, BLOCKS * MOST, merge_top, jnp.full((2 * N_CLS, 128), NEG, jnp.float32), unroll=4
        )

        def merge_sum(q, carry):
            total, true_score = carry
            sel = list_of == pick_ref[q]
            scaled = jnp.exp(slot_stats[q, 0:1, :] - local_top) * slot_stats[q, 1:2, :]
            return (
                total + jnp.where(sel, scaled, 0.0),
                true_score + jnp.where(sel, slot_stats[q, 2:3, :], 0.0),
            )

        zero = jnp.zeros((2 * N_CLS, 128), jnp.float32)
        local_sum, local_true = lax.fori_loop(0, BLOCKS * MOST, merge_sum, (zero, zero), unroll=4)
        for d in range(N_CLS):
            for i, array in enumerate((local_top, local_sum, local_true)):
                stats_ref[d, 2 * i : 2 * i + 2, :] = array[2 * d : 2 * d + 2, :]
            stats_ref[d, 6:8, :] = jnp.zeros((2, 128), jnp.float32)


def score_slots(src, images, class_rows, target, pick):
    slots = BLOCKS * MOST
    _, taxa, width = class_rows.shape
    return pl.pallas_call(
        score_kernel,
        grid_spec=pltpu.PrefetchScalarGridSpec(
            num_scalar_prefetch=1,
            grid=(BLOCKS,),
            in_specs=[
                *[
                    pl.BlockSpec((1, 128, width), lambda p, src, i=i: (src[MOST * p + i], 0, 0))
                    for i in range(MOST)
                ],
                pl.BlockSpec((1, taxa, width), lambda p, src: (p, 0, 0)),
                pl.BlockSpec((MOST, 1, 128), lambda p, src: (p, 0, 0)),
                pl.BlockSpec((slots, 1, 128), lambda p, src: (0, 0, 0)),
            ],
            out_specs=[
                pl.BlockSpec((MOST, taxa, 128), lambda p, src: (p, 0, 0)),
                pl.BlockSpec((MOST, 128, width), lambda p, src: (p, 0, 0)),
                pl.BlockSpec((N_CLS, 8, 128), lambda p, src: (0, 0, 0)),
            ],
            scratch_shapes=[pltpu.VMEM((slots, 8, 128), jnp.float32)],
        ),
        out_shape=[
            jax.ShapeDtypeStruct((slots, taxa, 128), jnp.float32),
            jax.ShapeDtypeStruct((slots, 128, width), jnp.bfloat16),
            jax.ShapeDtypeStruct((N_CLS, 8, 128), jnp.float32),
        ],
        name="score_slots",
    )(src, *([images] * MOST), class_rows, target, pick)


def grad_kernel(
    stats, target_ref, pick_ref, scores_in, picked_in, lse_ref, out_ref,
    scores, picked, recv, mine, probs, grad, pair, arrived, held,
    send_a, recv_a, send_b, recv_b, send_p, recv_p, send_r, recv_r, local,
):
    me = lax.axis_index("cls")
    dp = lax.axis_index("dp")
    z, core = dp // 2, dp % 2
    other = z * 2 + (1 - core)
    up, down = ((z + 1) % NZ) * 2 + core, ((z + NZ - 1) % NZ) * 2 + core
    barrier = pltpu.get_barrier_semaphore()

    def greet(step, carry):
        pl.semaphore_signal(barrier, inc=1, device_id={"cls": (me + step) % N_CLS})
        return carry

    lax.fori_loop(1, N_CLS, greet, 0)
    for target in (other, up, down):
        pl.semaphore_signal(barrier, inc=1, device_id={"dp": target})
    take_scores = pltpu.make_async_copy(scores_in, scores, local.at[0])
    take_picked = pltpu.make_async_copy(picked_in, picked, local.at[1])
    take_scores.start()
    take_picked.start()
    pl.semaphore_wait(barrier, N_CLS + 2)

    def part_copy(step):
        target = (me + step) % N_CLS
        return pltpu.make_async_remote_copy(
            src_ref=stats.at[target],
            dst_ref=recv.at[step],
            send_sem=send_a.at[step],
            recv_sem=recv_a.at[step],
            device_id={"cls": target},
        )

    def start_part(step, carry):
        part_copy(step).start()
        return carry

    def wait_part(step, carry):
        part_copy(step).wait()
        return carry

    lax.fori_loop(1, N_CLS, start_part, 0)
    recv[0] = stats[me]
    lax.fori_loop(1, N_CLS, wait_part, 0)

    parts = recv[...]
    tops = parts[:, 0:2, :]
    top = jnp.max(tops, axis=0)
    total = jnp.sum(jnp.exp(tops - top[None]) * parts[:, 2:4, :], axis=0)
    true_score = jnp.sum(parts[:, 4:6, :], axis=0)
    log_norm = top + jnp.log(total)
    mine[0:2, :] = log_norm
    mine[2:4, :] = log_norm - true_score
    mine[4:8, :] = jnp.zeros((4, 128), jnp.float32)
    lse_ref[me] = mine[...]

    def whole_copy(step):
        return pltpu.make_async_remote_copy(
            src_ref=mine,
            dst_ref=lse_ref.at[me],
            send_sem=send_b.at[step],
            recv_sem=recv_b.at[step],
            device_id={"cls": (me + step) % N_CLS},
        )

    def start_whole(step, carry):
        whole_copy(step).start()
        return carry

    def wait_whole(step, carry):
        whole_copy(step).wait()
        return carry

    lax.fori_loop(1, N_CLS, start_whole, 0)
    lax.fori_loop(1, N_CLS, wait_whole, 0)

    norms = jnp.concatenate([lse_ref[d, 0:2, :] for d in range(N_CLS)], axis=0)
    list_of = lax.broadcasted_iota(jnp.int32, (2 * N_CLS, 128), 0)
    taxon = lax.broadcasted_iota(jnp.int32, (256, 128), 0)
    take_scores.wait()
    take_picked.wait()

    def chunk_of(chain, step):
        if chain < BLOCKS // 2:
            return (z + NZ - 1 - step) % NZ
        return (z + 1 + step) % NZ

    def pair_copy(chain, step):
        return pltpu.make_async_remote_copy(
            src_ref=grad.at[chain, chunk_of(chain, step) * 2 + (1 - core)],
            dst_ref=pair.at[chain, step],
            send_sem=send_p.at[chain, step],
            recv_sem=recv_p.at[chain, step],
            device_id={"dp": other},
        )

    def ring_copy(chain, half, step):
        return pltpu.make_async_remote_copy(
            src_ref=held.at[chain, step, half],
            dst_ref=arrived.at[chain, step, half],
            send_sem=send_r.at[chain, step, half],
            recv_sem=recv_r.at[chain, step, half],
            device_id={"dp": up if chain < BLOCKS // 2 else down},
        )

    turn = [0, BLOCKS // 2, 1, BLOCKS // 2 + 1]
    for j in turn:
        for s in range(MOST):
            q = j * MOST + s
            pick = pick_ref[q]
            norm = jnp.sum(jnp.where(list_of == pick, norms, 0.0), axis=0, keepdims=True)
            prob = jnp.exp(scores[q] - norm)
            hot = (taxon == target_ref[q]).astype(jnp.float32)
            value = jnp.where(taxon + pick >= taxon, prob - hot, 0.0)
            probs[:, s * 128 : (s + 1) * 128] = value.astype(jnp.bfloat16)
        total = jnp.dot(
            probs[...],
            picked[j * MOST : (j + 1) * MOST].reshape(MOST * 128, picked.shape[2]),
            preferred_element_type=jnp.float32,
        )
        grad[j] = total.reshape(grad.shape[1:])
        for step in range(NZ):
            pair_copy(j, step).start()
    for step in range(NZ):
        for chain in turn:
            pair_copy(chain, step).wait_recv()
            for half in range(2):
                span = pl.ds(half * 8, 8)
                value = (
                    grad[chain, chunk_of(chain, step) * 2 + core, span, :]
                    + pair[chain, step, span, :]
                )
                if step > 0:
                    ring_copy(chain, half, step - 1).wait_recv()
                    value = value + arrived[chain, step - 1, half]
                if step < NZ - 1:
                    held[chain, step, half] = value
                    ring_copy(chain, half, step).start()
                else:
                    out_ref[chain, span, :] = value
    for step in range(NZ):
        for chain in turn:
            pair_copy(chain, step).wait_send()
            if step < NZ - 1:
                for half in range(2):
                    ring_copy(chain, half, step).wait_send()


def combine_and_scatter(stats, target, pick, scores, picked, shares):
    slots, taxa, _ = scores.shape
    width, share = picked.shape[2], taxa // shares
    vmem = pl.BlockSpec(memory_space=pltpu.VMEM)
    hbm = pl.BlockSpec(memory_space=pltpu.HBM)
    dma = pltpu.SemaphoreType.DMA
    return pl.pallas_call(
        grad_kernel,
        out_shape=[
            jax.ShapeDtypeStruct((N_CLS, 8, 128), jnp.float32),
            jax.ShapeDtypeStruct((BLOCKS, share, width), jnp.float32),
        ],
        in_specs=[vmem] * 3 + [hbm] * 2,
        out_specs=[vmem] * 2,
        scratch_shapes=[
            pltpu.VMEM((slots, taxa, 128), jnp.float32),
            pltpu.VMEM((slots, 128, width), jnp.bfloat16),
            pltpu.VMEM((N_CLS, 8, 128), jnp.float32),
            pltpu.VMEM((8, 128), jnp.float32),
            pltpu.VMEM((taxa, MOST * 128), jnp.bfloat16),
            pltpu.VMEM((BLOCKS, shares, share, width), jnp.float32),
            pltpu.VMEM((BLOCKS, NZ, share, width), jnp.float32),
            pltpu.VMEM((BLOCKS, NZ, 2, share // 2, width), jnp.float32),
            pltpu.VMEM((BLOCKS, NZ, 2, share // 2, width), jnp.float32),
            dma((N_CLS,)),
            dma((N_CLS,)),
            dma((N_CLS,)),
            dma((N_CLS,)),
            dma((BLOCKS, NZ)),
            dma((BLOCKS, NZ)),
            dma((BLOCKS, NZ, 2)),
            dma((BLOCKS, NZ, 2)),
            dma((2,)),
        ],
        compiler_params=pltpu.CompilerParams(
            collective_id=0, has_side_effects=True, vmem_limit_bytes=62 * 1024 * 1024
        ),
        name="combine_and_scatter",
    )(stats, target, pick, scores, picked)


def body(embeddings, class_rows, cand_blocks, label_pos):
    local_blocks, block_taxa, feature_width = class_rows.shape
    own_images, (own_lists, listed) = label_pos.shape[0], cand_blocks.shape
    small = jnp.concatenate([label_pos, cand_blocks.reshape(-1)])
    small = jnp.pad(small, (0, 8 * 128 - small.shape[0])).reshape(8, 128)
    gathered, small_all = gather_images(embeddings, small)
    gathered = gathered.reshape(N_CLS * own_images, feature_width)
    small_all = small_all.reshape(N_CLS, 8 * 128)
    labels_all = small_all[:, :own_images].reshape(-1)
    cand_all = small_all[:, own_images : own_images + own_lists * listed].reshape(-1, listed)
    group_lists = cand_all.shape[0]
    dp_images = gathered.shape[0]
    group_rows = dp_images // group_lists
    my_shard = lax.axis_index("cls")
    owned_ids = my_shard * local_blocks + jnp.arange(local_blocks, dtype=jnp.int32)
    matches = (cand_all[:, :, None] == owned_ids[None, None, :]).astype(jnp.int32)
    hit_count = jnp.sum(matches, axis=1)
    slot_of = jnp.sum(
        matches * jnp.arange(cand_all.shape[1], dtype=jnp.int32)[None, :, None], axis=1
    )
    hit_rank = jnp.cumsum(hit_count, axis=0) - 1
    slot_ids = jnp.arange(MOST, dtype=jnp.int32)
    chosen = (
        (hit_count[:, :, None] > 0) & (hit_rank[:, :, None] == slot_ids[None, None, :])
    ).astype(jnp.int32)
    block_index = jnp.arange(group_lists, dtype=jnp.int32)[:, None, None]
    src_block = jnp.sum(chosen * block_index, axis=0)
    valid_slot = jnp.sum(chosen, axis=0)
    src_slot = jnp.sum(chosen * slot_of[:, :, None], axis=0)
    valid = valid_slot.reshape(-1, 1) > 0
    label_tiles = labels_all.reshape(group_lists, group_rows)[src_block.reshape(-1)]
    target = jnp.where(valid, label_tiles - src_slot.reshape(-1, 1) * block_taxa, -1)
    pick = jnp.broadcast_to(jnp.where(valid, src_block.reshape(-1, 1), -1), target.shape)
    target, pick = target[:, None, :], pick[:, None, :]
    scores, picked, stats = score_slots(
        src_block.reshape(-1), gathered.reshape(group_lists, group_rows, feature_width), class_rows, target, pick
    )
    combined, grad = combine_and_scatter(stats, target, pick, scores, picked, lax.axis_size("dp"))
    per = group_lists // N_CLS
    image_loss = combined[:, per : 2 * per].reshape(dp_images)
    class_grad = grad.transpose(1, 0, 2)
    return (image_loss, class_grad)


def solution(mesh):
    in_specs = (
        P(("dp", "cls"), None),
        P("cls", None, None),
        P(("dp", "cls"), None),
        P(("dp", "cls")),
    )
    out_specs = (P("dp"), P("dp", "cls", None))
    return jax.shard_map(body, mesh=mesh, in_specs=in_specs, out_specs=out_specs, check_vma=False)
```
